128 devices in a mesh: seq: 32 (over y, x, core), tp: 4 (over z).
Axes of the slice: x: 4, y: 4, z: 4, core: 2. Of those that a mesh axis runs over, the one named last changes fastest.
Arguments:
- codes: bfloat16 [16384, 4096], P('seq', 'tp'), may hold values from -127 to 127, as said below
- exponents: int32 [16384], P('seq'), may hold values from -8 to -5
- w_query: bfloat16 [4096, 4096], P(None, 'tp'), may hold values from -0.09375 to 0.09375
- w_key: bfloat16 [4096, 4096], P(None, 'tp'), may hold values from -0.09375 to 0.09375
- w_value: bfloat16 [4096, 4096], P(None, 'tp'), may hold values from -0.09375 to 0.09375
- norm_gain: float32 [4096], P('tp'), may hold values from 0.1 to 1.9
- w_out: bfloat16 [4096, 4096], P('tp'), may hold values from -0.09375 to 0.09375
Outputs:
- mixed: bfloat16 [16384, 4096], P(('seq', 'tp'))
The draws below stay inside these ranges and needn't reach their ends.
Inputs may be any that keep to these rules, and one draw needn't show every extreme that they name: `codes`: every entry is a whole number.
All inputs are finite; a program needn't handle non-finite values.
Results may differ from the reference program's by a relative error of at most 0.012.
Values may be sent and summed in bfloat16 or wider, within the bound.
No kernel may reach another device: no remote copies, remote signals or barrier semaphores. Data moves between devices by JAX's collectives and lax.ppermute only.
A program may use at most 128 MiB of HBM per device.

```python
import jax
import jax.numpy as jnp
from jax import lax

D = 4096
H = 32
HD = 128
BLK = 512
TOKENS = 16384


def draw_codes(key, part):
    whole = jax.random.randint(key, (TOKENS, D), -127, 128)
    return whole.astype(jnp.float32).astype(jnp.bfloat16)


def touch_ends(drawn, stream_key, least, top_value):
    spot = [jax.random.randint(jax.random.fold_in(stream_key, axis), (), 0, length) for axis, length in enumerate(drawn.shape)]
    main_axis = drawn.shape.index(max(drawn.shape))
    beside = spot[:main_axis] + [(spot[main_axis] + 1) % drawn.shape[main_axis]] + spot[main_axis + 1:]
    return drawn.at[tuple(spot)].set(least).at[tuple(beside)].set(top_value)


def level_of(rng, dims, cuts, least, largest):
    level, own = 1.0, jax.random.fold_in(rng, 6)
    for axis_at, shards_of in cuts:
        steps = jnp.exp(jax.random.uniform(jax.random.fold_in(own, axis_at), (shards_of,), jnp.float32, least / len(cuts), largest / len(cuts)))
        level = level * jnp.repeat(steps, dims[axis_at] // shards_of).reshape([-1 if axis == axis_at else 1 for axis in range(len(dims))])
    return level


def bell_draw(rng, dims, spread, limit, split=(), held_as=jnp.bfloat16):
    entries = jax.random.normal(rng, dims, jnp.float32) * spread
    if len(split) > 0:
        entries = level_of(rng, dims, split, -0.22, 0.18) * entries
    return jnp.clip(entries, min=-limit, max=limit).astype(held_as)


def setup_inputs(seed: int = 0) -> dict:
    keys = jax.random.split(jax.random.key(seed), 8)
    return {
        "codes": draw_codes(jax.random.fold_in(keys[7], 71), 0),
        "exponents": touch_ends(jax.random.randint(keys[1], (TOKENS,), -8, -4), jax.random.fold_in(keys[1], 1), -8, (-4) - 1).astype(jnp.int32),
        "w_query": bell_draw(keys[2], (D, H * HD), D ** -0.5, 0.09375, ((1, 4),)),
        "w_key": bell_draw(keys[3], (D, H * HD), D ** -0.5, 0.09375, ((1, 4),)),
        "w_value": bell_draw(keys[4], (D, H * HD), D ** -0.5, 0.09375, ((1, 4),)),
        "norm_gain": jnp.clip(1.0 + 0.18 * jax.random.normal(keys[5], (H * HD,), jnp.float32), 0.1, 1.9),
        "w_out": bell_draw(keys[6], (H * HD, D), (H * HD) ** -0.5, 0.09375, ((0, 4),)),
    }


def reference(codes, exponents, w_query, w_key, w_value, norm_gain, w_out):
    blocks = codes.shape[0] // BLK
    causal = jnp.tril(jnp.ones((BLK, BLK), jnp.float32))
    gain = norm_gain.reshape(H, HD)

    def step(state, index):
        start = (index * BLK).astype(jnp.int32)
        block_codes = lax.dynamic_slice_in_dim(codes, start, BLK, 0).astype(jnp.float32)
        block_exps = lax.dynamic_slice_in_dim(exponents, start, BLK, 0).astype(jnp.float32)
        x = (block_codes * jnp.exp2(block_exps)[:, None]).astype(jnp.bfloat16)
        q = jnp.dot(x, w_query, preferred_element_type=jnp.float32)
        k = jnp.dot(x, w_key, preferred_element_type=jnp.float32)
        v = jnp.dot(x, w_value, preferred_element_type=jnp.float32)
        feat_q = (jax.nn.elu(q) + 1.0).astype(jnp.bfloat16).astype(jnp.float32).reshape(BLK, H, HD)
        feat_k = (jax.nn.elu(k) + 1.0).astype(jnp.bfloat16).astype(jnp.float32).reshape(BLK, H, HD)
        values = v.astype(jnp.bfloat16).astype(jnp.float32).reshape(BLK, H, HD)
        state_b = state.astype(jnp.bfloat16).astype(jnp.float32)
        inter = jnp.einsum('shd,hde->she', feat_q, state_b, precision=lax.Precision.HIGHEST)
        scores = jnp.einsum('shd,thd->hst', feat_q, feat_k, precision=lax.Precision.HIGHEST) * causal[None]
        scores = scores.astype(jnp.bfloat16).astype(jnp.float32)
        intra = jnp.einsum('hst,the->she', scores, values, precision=lax.Precision.HIGHEST)
        y = inter + intra
        mean_sq = lax.optimization_barrier(jnp.mean(y * y, axis=-1, keepdims=True))
        normed = (y * lax.rsqrt(mean_sq + 1e-05) * gain[None]).astype(jnp.bfloat16).reshape(BLK, H * HD)
        out = jnp.dot(normed, w_out, preferred_element_type=jnp.float32).astype(jnp.bfloat16)
        state = state + jnp.einsum('shd,she->hde', feat_k, values, precision=lax.Precision.HIGHEST)
        return (state, out)
    init = jnp.zeros((H, HD, HD), jnp.float32)
    final, outs = lax.scan(step, init, jnp.arange(blocks, dtype=jnp.int32))
    return outs.reshape(blocks * BLK, w_out.shape[1])
```

```python
import jax
import jax.numpy as jnp
from jax import lax
from jax.sharding import PartitionSpec as P

HD = 128
BLK = 512


def ring(n, d):
    return [(i, (i + d) % n) for i in range(n)]


def chip(y, x, c):
    return (y * 4 + x) * 2 + c


def pairs(k, first):
    found = []
    for y in range(4):
        for x in range(4):
            for c in range(2):
                along_y = (c == 0) == first
                if along_y and y + k < 4:
                    found.append((chip(y, x, c), chip(y + k, x, c)))
                if not along_y:
                    found.append((chip(y, x, c), chip(y, (x + k) % 4, c)))
    return found


SWAP = [(s, s ^ 1) for s in range(32)]
f32 = jnp.float32
bf16 = jnp.bfloat16


def before_this(state):
    s = lax.axis_index("seq")
    c, x = s % 2, (s // 2) % 4
    core0 = c == 0
    half = state.shape[0] // 2
    mine = lax.dynamic_slice_in_dim(state, c * half, half, 0)
    other = lax.dynamic_slice_in_dim(state, (1 - c) * half, half, 0)
    theirs = lax.ppermute(other.astype(bf16), "seq", SWAP).astype(f32)
    both = mine + theirs
    sent = both.astype(bf16)
    r = [lax.ppermute(sent, "seq", pairs(k, True)).astype(f32) for k in (1, 2, 3)]
    total = r[0] + r[1] + r[2]
    row = jnp.zeros_like(total)
    for k in (1, 2, 3):
        row = row + jnp.where(x >= k, r[k - 1], 0.0)
    got = []
    for k in (1, 2, 3):
        keep = jnp.where(core0, (x + k < 4), True)
        v = (total + jnp.where(keep, both, 0.0)).astype(bf16)
        got.append(lax.ppermute(v, "seq", pairs(k, False)).astype(f32))
    prefix = jnp.where(core0, total, row) + got[0] + got[1] + got[2]
    own = prefix + jnp.where(core0, 0.0, theirs)
    partner = prefix + jnp.where(core0, mine, 0.0)
    back = lax.ppermute(partner.astype(bf16), "seq", SWAP)
    own = own.astype(bf16)
    low = jnp.where(core0, own, back)
    high = jnp.where(core0, back, own)
    return jnp.concatenate([low, high], 0)


def on_device(codes, exponents, w_query, w_key, w_value, norm_gain, w_out):
    z = lax.axis_index("tp")
    tok, part = codes.shape
    hp = part // 2
    width = w_query.shape[1]
    heads = width // HD
    row_scale = jnp.exp2(exponents.astype(f32))[:, None]
    up, down = ring(4, 1), ring(4, -1)

    a, b = codes[:, :hp], codes[:, hp:]
    a_left = lax.ppermute(a, "tp", up)
    b_right = lax.ppermute(b, "tp", down)
    b_left = lax.ppermute(b, "tp", up)
    a_right = lax.ppermute(a, "tp", down)
    a_far = lax.ppermute(a_left, "tp", up)
    b_far = lax.ppermute(b_right, "tp", down)
    lz, rz, fz = (z + 3) % 4, (z + 1) % 4, (z + 2) % 4
    pieces = (
        (codes, z * part),
        (a_left, lz * part),
        (b_right, rz * part + hp),
        (b_left, lz * part + hp),
        (a_right, rz * part),
        (a_far, fz * part),
        (b_far, fz * part + hp),
    )

    def project(w):
        acc = None
        for piece, start in pieces:
            rows = lax.dynamic_slice_in_dim(w, start, piece.shape[1], 0)
            term = jnp.dot(piece, rows, preferred_element_type=f32)
            acc = term if acc is None else acc + term
        return acc * row_scale

    feat_k = (jax.nn.elu(project(w_key)) + 1.0).astype(bf16).reshape(tok, heads, HD)
    value_b = project(w_value).astype(bf16).reshape(tok, heads, HD)
    state = jnp.einsum("shd,she->hde", feat_k, value_b, preferred_element_type=f32)
    before = before_this(state)
    feat_q = (jax.nn.elu(project(w_query)) + 1.0).astype(bf16).reshape(tok, heads, HD)
    causal = jnp.tril(jnp.ones((BLK, BLK), f32))
    scores = jnp.einsum("shd,thd->hst", feat_q, feat_k, preferred_element_type=f32)
    scores = (scores * causal[None]).astype(bf16)
    intra = jnp.einsum("hst,the->she", scores, value_b, preferred_element_type=f32)
    inter = jnp.einsum("shd,hde->she", feat_q, before, preferred_element_type=f32)
    y = inter + intra
    mean_sq = jnp.mean(y * y, axis=-1, keepdims=True)
    gain = norm_gain.reshape(heads, HD)
    o = (y * lax.rsqrt(mean_sq + 1e-05) * gain).astype(bf16).reshape(tok, width)

    quarter = tok // 4
    hw = w_out.shape[1] // 2

    def share(chunk, side):
        rows = lax.dynamic_slice_in_dim(o, chunk * quarter, quarter, 0)
        w = w_out[:, :hw] if side == 0 else w_out[:, hw:]
        return jnp.dot(rows, w, preferred_element_type=f32)

    u_pass = lax.ppermute(share(fz, 0).astype(bf16), "tp", up)
    l_pass = lax.ppermute(share(fz, 1).astype(bf16), "tp", down)
    l_low = lax.ppermute(share(rz, 1).astype(bf16), "tp", up)
    u_high = lax.ppermute(share(lz, 0).astype(bf16), "tp", down)
    u_low = lax.ppermute((share(rz, 0) + u_pass.astype(f32)).astype(bf16), "tp", up)
    l_high = lax.ppermute((share(lz, 1) + l_pass.astype(f32)).astype(bf16), "tp", down)
    u = share(z, 0) + u_high.astype(f32) + u_low.astype(f32)
    l = share(z, 1) + l_low.astype(f32) + l_high.astype(f32)
    return jnp.concatenate([u, l], 1).astype(bf16)


def solution(mesh):
    in_specs = (
        P("seq", "tp"),
        P("seq"),
        P(None, "tp"),
        P(None, "tp"),
        P(None, "tp"),
        P("tp"),
        P("tp", None),
    )
    out_specs = P(("seq", "tp"), None)
    return jax.shard_map(
        on_device, mesh=mesh, in_specs=in_specs, out_specs=out_specs, check_vma=False
    )
```

```python
import functools

import jax
import jax.numpy as jnp
from jax import lax
from jax.experimental import pallas as pl
from jax.experimental.pallas import tpu as pltpu
from jax.sharding import PartitionSpec as P

HD = 128
BLK = 512
TN = 256
MIB = 1 << 20


f32 = jnp.float32
bf16 = jnp.bfloat16
HBM = pl.BlockSpec(memory_space=pltpu.HBM)
VM = pl.BlockSpec(memory_space=pltpu.VMEM)


def ring(n, d):
    return [(i, (i + d) % n) for i in range(n)]


def chip(y, x, c):
    return (y * 4 + x) * 2 + c


def exchange(move, first):
    found = []
    for y in range(4):
        for x in range(4):
            for c in range(2):
                along_y = (c == 0) == first
                to = (move(y), x, c) if along_y else (y, move(x), c)
                found.append((chip(y, x, c), chip(*to)))
    return found


SWAP = [(s, s ^ 1) for s in range(32)]


def near(v):
    return v ^ 1


def mirror(v):
    return 3 - v


def shift(v, pairs, axis="tp"):
    return lax.ppermute(v, axis, pairs)


def in_hbm(*arrays):
    return [pltpu.with_memory_space_constraint(v, pltpu.HBM) for v in arrays]


def dot(a, b):
    return jnp.dot(a, b, preferred_element_type=f32)


def params(limit, **more):
    return pltpu.CompilerParams(vmem_limit_bytes=limit * MIB, **more)


def cost(flops, nbytes):
    return pl.CostEstimate(flops=flops, bytes_accessed=nbytes, transcendentals=0)


OWN, LEFT, RIGHT, FAR, CORE0, ODD_A, HIGH_A, ODD_B, HIGH_B = range(9)
SCALARS = pl.BlockSpec(memory_space=pltpu.SMEM)


def project_kernel(count, have, info, *refs):
    xs, refs = refs[:count], refs[count:]
    ws, refs = refs[: 3 * count], refs[3 * count :]
    accs, outs = (refs[:3], refs[3:]) if have else (None, refs)
    cols = pl.ds(pl.multiple_of(pl.program_id(0) * TN, TN), TN)
    for i in range(3):
        total = accs[i][:, cols] if have else None
        for j in range(count):
            term = dot(xs[j][...], ws[3 * j + i][...])
            total = term if total is None else total + term
        outs[i][:, cols] = total


def project(info, pieces, blocks, weights, accs):
    count, have = len(pieces), accs is not None
    tok, depth = pieces[0].shape
    width = weights[0].shape[1]

    def wspec(j):
        device, half = blocks[j]
        return pl.BlockSpec((depth, TN), lambda n, i: (2 * i[device] + half, n))

    return pl.pallas_call(
        functools.partial(project_kernel, count, have),
        out_shape=[pltpu.VMEM((tok, width), f32)] * 3,
        grid_spec=pltpu.PrefetchScalarGridSpec(
            num_scalar_prefetch=1,
            grid=(width // TN,),
            in_specs=[VM] * count
            + [wspec(j) for j in range(count) for _ in range(3)]
            + ([VM] * 3 if have else []),
            out_specs=[VM] * 3,
        ),
        compiler_params=params(16),
        cost_estimate=cost(6 * count * tok * depth * width, 6 * count * depth * width),
    )(info, *pieces, *(list(weights) * count), *(accs or ()))


def fetch_kernel(rows, info, wq, wk, wv, wo, fq, fk, fv, fo, sem):
    start = pl.multiple_of(info[FAR] * rows, rows)
    copies = [
        pltpu.make_async_copy(w.at[pl.ds(start, rows), :], f, sem.at[n])
        for n, (w, f) in enumerate(((wk, fk), (wv, fv), (wq, fq)))
    ]
    copies.append(pltpu.make_async_copy(wo, fo, sem.at[3]))
    for c in copies:
        c.start()
    for c in copies:
        c.wait()


def fetch(info, rows, weights, w_out):
    width = weights[0].shape[1]
    return pl.pallas_call(
        functools.partial(fetch_kernel, rows),
        out_shape=[pltpu.VMEM((rows, width), bf16)] * 3 + [pltpu.VMEM(w_out.shape, bf16)],
        in_specs=[SCALARS] + [HBM] * 4,
        out_specs=[VM] * 4,
        scratch_shapes=[pltpu.SemaphoreType.DMA((4,))],
        compiler_params=params(8),
        cost_estimate=cost(0, 14 * MIB),
    )(info, *weights, w_out)


def feature(t):
    return jnp.where(t > 0, t + 1.0, jnp.exp(t)).astype(bf16)


def last_kv_kernel(info, xa, xb, wk, wv, acck, accv, scale, fk, vb, mine, other, state):
    half = xa.shape[1]

    @pl.loop(0, fk.shape[1] // TN)
    def _(n):
        cols = pl.ds(pl.multiple_of(n * TN, TN), TN)

        def full(w, acc):
            t = acc[:, cols] + dot(xa[...], w[pl.ds(0, half), cols])
            return (t + dot(xb[...], w[pl.ds(half, half), cols])) * scale[...]

        k = feature(full(wk, acck))
        v = full(wv, accv).astype(bf16)
        fk[:, cols] = k
        vb[:, cols] = v
        for h in range(TN // HD):
            part = slice(h * HD, (h + 1) * HD)
            state[n * (TN // HD) + h] = lax.dot_general(
                k[:, part], v[:, part], (((0,), (0,)), ((), ())), preferred_element_type=f32
            )

    count = mine.shape[0]
    for h in range(count):
        mine[h] = state[(1 - info[CORE0]) * count + h]
        other[h] = state[info[CORE0] * count + h].astype(bf16)


def last_kv(info, xa, xb, wk, wv, acck, accv, scale):
    tok, width = acck.shape
    return pl.pallas_call(
        last_kv_kernel,
        out_shape=[
            pltpu.VMEM((tok, width), bf16),
            pltpu.VMEM((tok, width), bf16),
            pltpu.VMEM((width // HD // 2, HD, HD), f32),
            pltpu.VMEM((width // HD // 2, HD, HD), bf16),
        ],
        in_specs=[SCALARS] + [VM] * 7,
        out_specs=[VM] * 4,
        scratch_shapes=[pltpu.VMEM((width // HD, HD, HD), f32)],
        compiler_params=params(12),
        cost_estimate=cost(4 * tok * 1024 * width, 8 * MIB),
    )(info, xa, xb, wk, wv, acck, accv, scale)


def last_q_kernel(xa, xb, w, acc, scale, fq):
    half = xa.shape[1]

    @pl.loop(0, fq.shape[1] // TN)
    def _(n):
        cols = pl.ds(pl.multiple_of(n * TN, TN), TN)
        t = acc[:, cols] + dot(xa[...], w[pl.ds(0, half), cols])
        fq[:, cols] = feature((t + dot(xb[...], w[pl.ds(half, half), cols])) * scale[...])


def last_q(xa, xb, w, acc, scale):
    tok, width = acc.shape
    return pl.pallas_call(
        last_q_kernel,
        out_shape=pltpu.VMEM((tok, width), bf16),
        in_specs=[VM] * 5,
        out_specs=VM,
        compiler_params=params(12),
        cost_estimate=cost(2 * tok * 1024 * width, 4 * MIB),
    )(xa, xb, w, acc, scale)


def within_kernel(first, fq, fk, vb, out):
    rows = BLK // 2
    row = lax.broadcasted_iota(jnp.int32, (rows, rows), 0)
    col = lax.broadcasted_iota(jnp.int32, (rows, rows), 1)
    keep = row >= col

    @pl.loop(0, out.shape[1] // HD)
    def _(h):
        cols = pl.ds(pl.multiple_of((first + h) * HD, HD), HD)
        ocols = pl.ds(pl.multiple_of(h * HD, HD), HD)

        def scores(q, k):
            return lax.dot_general(
                q, k, (((1,), (1,)), ((), ())), preferred_element_type=f32
            )

        for i in range(2):
            mine = pl.ds(i * rows, rows)
            q = fq[mine, cols]
            s = jnp.where(keep, scores(q, fk[mine, cols]), 0.0).astype(bf16)
            y = dot(s, vb[mine, cols])
            if i == 1:
                early = pl.ds(0, rows)
                s = scores(q, fk[early, cols]).astype(bf16)
                y = y + dot(s, vb[early, cols])
            out[mine, ocols] = y


def within(first, heads, fq, fk, vb):
    tok = fq.shape[0]
    return pl.pallas_call(
        functools.partial(within_kernel, first),
        out_shape=pltpu.VMEM((tok, heads * HD), f32),
        in_specs=[VM] * 3,
        out_specs=VM,
        compiler_params=params(12),
        cost_estimate=cost(4 * heads * tok * tok * HD, 4 * MIB),
    )(fq, fk, vb)


def share_kernel(place, sides, heads, info, fq, ylow, yhigh, own, back, gain, wo, *refs):
    outs, o = refs[:-1], refs[-1]
    rows = o.shape[0]
    mine = pl.ds(pl.multiple_of(info[place] * rows, rows), rows)
    for h in range(heads):
        cols = slice(h * HD, (h + 1) * HD)
        near_y = ylow if h < heads // 2 else yhigh
        g = h % (heads // 2)
        took = own if h < heads // 2 else back
        gave = back if h < heads // 2 else own
        state = jnp.where(info[CORE0] == 1, took[g], gave[g])
        y = near_y[mine, g * HD : (g + 1) * HD] + dot(fq[mine, cols], state)
        ms = jnp.mean(y * y, axis=-1, keepdims=True)
        o[:, cols] = (y * lax.rsqrt(ms + 1e-05) * gain[:, cols]).astype(bf16)
    half = wo.shape[1] // 2
    for side, out in zip(sides, outs):

        @pl.loop(0, half // 512)
        def _(n):
            src = pl.ds(pl.multiple_of(side * half + n * 512, 512), 512)
            dst = pl.ds(pl.multiple_of(n * 512, 512), 512)
            out[:, dst] = dot(o[...], wo[:, src]).astype(out.dtype)


def share(info, place, sides, types, fq, ylow, yhigh, own, back, gain, wo):
    tok, width = fq.shape
    rows, half = tok // 4, wo.shape[1] // 2
    return pl.pallas_call(
        functools.partial(share_kernel, place, sides, width // HD),
        out_shape=[pltpu.VMEM((rows, half), t) for t in types],
        in_specs=[SCALARS] + [VM] * 7,
        out_specs=[VM] * len(sides),
        scratch_shapes=[pltpu.VMEM((rows, width), bf16)],
        compiler_params=params(12),
        cost_estimate=cost(2 * rows * width * half * len(sides), 4 * MIB),
    )(info, fq, ylow, yhigh, own, back, gain, wo)


def small(body, outs, info, *ins):
    def kernel(info, *refs):
        flag = [info[n].astype(f32) for n in range(info.shape[0])]
        for h in range(refs[0].shape[0]):
            got = [r[h].astype(f32) for r in refs[: len(ins)]]
            for ref, value in zip(refs[len(ins) :], body(flag, *got)):
                ref[h] = value.astype(ref.dtype)

    count = ins[0].shape[0]
    return pl.pallas_call(
        kernel,
        out_shape=[pltpu.VMEM((count, HD, HD), t) for t in outs],
        in_specs=[SCALARS] + [VM] * len(ins),
        out_specs=[VM] * len(outs),
        compiler_params=params(4),
        cost_estimate=cost(1000, MIB // 2),
    )(info, *ins)


def before_this(info, mine, other):
    def send(v, pairs):
        return shift(v, pairs, "seq")

    theirs = send(other, SWAP)
    (both,) = small(lambda i, m, t: (m + t,), (bf16,), info, mine, theirs)
    r1 = send(both, exchange(near, True))
    (two,) = small(lambda i, m, t, r1: (m + t + r1,), (bf16,), info, mine, theirs, r1)
    r2 = send(two, exchange(mirror, True))

    def third(i, m, t, r1, r2):
        earlier = i[ODD_A] * r1 + i[HIGH_A] * r2
        four = m + t + r1 + r2
        first = i[CORE0] * earlier + (1.0 - i[CORE0]) * four
        return earlier, first, first

    earlier, first, sent = small(third, (f32, f32, bf16), info, mine, theirs, r1, r2)
    r3 = send(sent, exchange(near, False))
    t3 = send(both, exchange(near, False))

    def fourth(i, earlier, first, r3, t3, m, t):
        v = first + r3 + i[CORE0] * (1.0 - i[HIGH_B]) * (m + t + t3)
        seen = i[CORE0] + (1.0 - i[CORE0]) * i[ODD_B]
        return v, earlier + seen * r3 + i[CORE0] * i[ODD_B] * t3

    v, earlier = small(fourth, (bf16, f32), info, earlier, first, r3, t3, mine, theirs)
    r4 = send(v, exchange(mirror, False))

    def fifth(i, earlier, r4, m, t):
        before = earlier + (i[CORE0] + (1.0 - i[CORE0]) * i[HIGH_B]) * r4
        return before + (1.0 - i[CORE0]) * t, before + i[CORE0] * m

    own, partner = small(fifth, (bf16, bf16), info, earlier, r4, mine, theirs)
    return own, send(partner, SWAP)


def on_device(codes, exponents, w_query, w_key, w_value, norm_gain, w_out):
    z = lax.axis_index("tp")
    s = lax.axis_index("seq")
    core, x, y = s % 2, (s // 2) % 4, s // 8
    first, second = jnp.where(core == 0, y, x), jnp.where(core == 0, x, y)
    info = jnp.stack(
        [
            z,
            (z + 3) % 4,
            (z + 1) % 4,
            (z + 2) % 4,
            1 - core,
            first % 2,
            first // 2,
            second % 2,
            second // 2,
        ]
    ).astype(jnp.int32)
    _, part = codes.shape
    hp = part // 2
    width = w_query.shape[1]
    heads = width // HD
    scale = jnp.exp2(exponents.astype(f32))[:, None]
    gain = norm_gain.reshape(1, width)
    codes, info, scale, gain = lax.optimization_barrier((codes, info, scale, gain))
    up, down = ring(4, 1), ring(4, -1)
    weights, w_out = in_hbm(w_query, w_key, w_value), in_hbm(w_out)[0]

    a, b = codes[:, :hp], codes[:, hp:]
    a_left = shift(a, up)
    b_right = shift(b, down)
    b_left = shift(b, up)
    a_right = shift(a, down)
    a_far = shift(a_left, up)
    b_far = shift(b_right, down)

    accs = project(info, (a, b), ((OWN, 0), (OWN, 1)), weights, None)
    wq_far, wk_far, wv_far, wo = fetch(info, part, weights, w_out)
    accs = project(info, (a_left, b_right), ((LEFT, 0), (RIGHT, 1)), weights, accs)
    accs = project(info, (b_left, a_right), ((LEFT, 1), (RIGHT, 0)), weights, accs)
    feat_k, value_b, mine, other = last_kv(
        info, a_far, b_far, wk_far, wv_far, accs[1], accs[2], scale
    )
    own, back = before_this(info, mine, other)
    feat_q = last_q(a_far, b_far, wq_far, accs[0], scale)
    ylow = within(0, heads // 2, feat_q, feat_k, value_b)
    yhigh = within(heads // 2, heads // 2, feat_q, feat_k, value_b)

    rest = (feat_q, ylow, yhigh, own, back, gain, wo)
    (u_far,) = share(info, FAR, (0,), (bf16,), *rest)
    u_pass = shift(u_far, up)
    (l_far,) = share(info, FAR, (1,), (bf16,), *rest)
    l_pass = shift(l_far, down)
    l_next, u_next = share(info, RIGHT, (1, 0), (bf16, f32), *rest)
    l_low = shift(l_next, up)
    u_prev, l_prev = share(info, LEFT, (0, 1), (bf16, f32), *rest)
    u_high = shift(u_prev, down)
    u, l = share(info, OWN, (0, 1), (f32, f32), *rest)
    u_low = shift((u_next + u_pass.astype(f32)).astype(bf16), up)
    l_high = shift((l_prev + l_pass.astype(f32)).astype(bf16), down)
    u = u + u_high.astype(f32) + u_low.astype(f32)
    l = l + l_low.astype(f32) + l_high.astype(f32)
    return jnp.concatenate([u, l], 1).astype(bf16)


def solution(mesh):
    in_specs = (
        P("seq", "tp"),
        P("seq"),
        P(None, "tp"),
        P(None, "tp"),
        P(None, "tp"),
        P("tp"),
        P("tp", None),
    )
    out_specs = P(("seq", "tp"), None)

    return jax.shard_map(
        on_device, mesh=mesh, in_specs=in_specs, out_specs=out_specs, check_vma=False
    )
```

```python
import functools

import jax
import jax.numpy as jnp
from jax import lax
from jax.experimental import pallas as pl
from jax.experimental.pallas import tpu as pltpu
from jax.sharding import PartitionSpec as P

HD = 128
BLK = 512
TN = 256
MIB = 1 << 20


f32 = jnp.float32
bf16 = jnp.bfloat16
HBM = pl.BlockSpec(memory_space=pltpu.HBM)
VM = pl.BlockSpec(memory_space=pltpu.VMEM)


def ring(n, d):
    return [(i, (i + d) % n) for i in range(n)]


def chip(y, x, c):
    return (y * 4 + x) * 2 + c


def exchange(move, first):
    found = []
    for y in range(4):
        for x in range(4):
            for c in range(2):
                along_y = (c == 0) == first
                to = (move(y), x, c) if along_y else (y, move(x), c)
                found.append((chip(y, x, c), chip(*to)))
    return found


SWAP = [(s, s ^ 1) for s in range(32)]


def near(v):
    return v ^ 1


def mirror(v):
    return 3 - v


def shift(v, pairs, axis="tp"):
    return lax.ppermute(v, axis, pairs)


def in_hbm(*arrays):
    return [pltpu.with_memory_space_constraint(v, pltpu.HBM) for v in arrays]


def dot(a, b):
    return jnp.dot(a, b, preferred_element_type=f32)


def params(limit, **more):
    return pltpu.CompilerParams(vmem_limit_bytes=limit * MIB, **more)


def cost(flops, nbytes):
    return pl.CostEstimate(flops=flops, bytes_accessed=nbytes, transcendentals=0)


OWN, LEFT, RIGHT, FAR, CORE0 = range(5)
SCALARS = pl.BlockSpec(memory_space=pltpu.SMEM)


def project_kernel(count, have, info, *refs):
    xs, refs = refs[:count], refs[count:]
    ws, refs = refs[: 3 * count], refs[3 * count :]
    accs, outs = (refs[:3], refs[3:]) if have else (None, refs)
    cols = pl.ds(pl.multiple_of(pl.program_id(0) * TN, TN), TN)
    for i in range(3):
        total = accs[i][:, cols] if have else None
        for j in range(count):
            term = dot(xs[j][...], ws[3 * j + i][...])
            total = term if total is None else total + term
        outs[i][:, cols] = total


def project(info, pieces, blocks, weights, accs):
    count, have = len(pieces), accs is not None
    tok, depth = pieces[0].shape
    width = weights[0].shape[1]

    def wspec(j):
        device, half = blocks[j]
        return pl.BlockSpec((depth, TN), lambda n, i: (2 * i[device] + half, n))

    return pl.pallas_call(
        functools.partial(project_kernel, count, have),
        out_shape=[pltpu.VMEM((tok, width), f32)] * 3,
        grid_spec=pltpu.PrefetchScalarGridSpec(
            num_scalar_prefetch=1,
            grid=(width // TN,),
            in_specs=[VM] * count
            + [wspec(j) for j in range(count) for _ in range(3)]
            + ([VM] * 3 if have else []),
            out_specs=[VM] * 3,
        ),
        compiler_params=params(16),
        cost_estimate=cost(6 * count * tok * depth * width, 6 * count * depth * width),
    )(info, *pieces, *(list(weights) * count), *(accs or ()))


def split_kernel(codes, a, b, sem):
    half = a.shape[1]
    copies = [
        pltpu.make_async_copy(codes.at[:, pl.ds(0, half)], a, sem.at[0]),
        pltpu.make_async_copy(codes.at[:, pl.ds(half, half)], b, sem.at[1]),
    ]
    for c in copies:
        c.start()
    for c in copies:
        c.wait()


def split(codes):
    tok, part = codes.shape
    return pl.pallas_call(
        split_kernel,
        out_shape=[pltpu.VMEM((tok, part // 2), bf16)] * 2,
        in_specs=[HBM],
        out_specs=[VM] * 2,
        scratch_shapes=[pltpu.SemaphoreType.DMA((2,))],
        compiler_params=params(4),
        cost_estimate=cost(0, 2 * MIB),
    )(codes)


def fetch_kernel(rows, info, wq, wk, wv, wo, fq, fk, fv, fo, sem):
    start = pl.multiple_of(info[FAR] * rows, rows)
    copies = [
        pltpu.make_async_copy(w.at[pl.ds(start, rows), :], f, sem.at[n])
        for n, (w, f) in enumerate(((wk, fk), (wv, fv), (wq, fq)))
    ]
    copies.append(pltpu.make_async_copy(wo, fo, sem.at[3]))
    for c in copies:
        c.start()
    for c in copies:
        c.wait()


def fetch(info, rows, weights, w_out):
    width = weights[0].shape[1]
    return pl.pallas_call(
        functools.partial(fetch_kernel, rows),
        out_shape=[pltpu.VMEM((rows, width), bf16)] * 3 + [pltpu.VMEM(w_out.shape, bf16)],
        in_specs=[SCALARS] + [HBM] * 4,
        out_specs=[VM] * 4,
        scratch_shapes=[pltpu.SemaphoreType.DMA((4,))],
        compiler_params=params(8),
        cost_estimate=cost(0, 14 * MIB),
    )(info, *weights, w_out)


def feature(t):
    return jnp.where(t > 0, t + 1.0, jnp.exp(t)).astype(bf16)


def last_kv_kernel(part, info, xa, xb, wk, wv, acck, accv, scale, fk, vb, state):
    half, width = xa.shape[1], fk.shape[1]
    core = 1 - info[CORE0]
    start = (core if part == 0 else 1 - core) * width

    for n in range(width // TN):
        cols = pl.ds(pl.multiple_of(start + n * TN, TN), TN)
        ocols = slice(n * TN, (n + 1) * TN)

        def full(w, acc):
            t = acc[:, cols] + dot(xa[...], w[pl.ds(0, half), cols])
            return (t + dot(xb[...], w[pl.ds(half, half), cols])) * scale[...]

        k = feature(full(wk, acck))
        v = full(wv, accv).astype(bf16)
        fk[:, ocols] = k
        vb[:, ocols] = v
        for h in range(TN // HD):
            cut = slice(h * HD, (h + 1) * HD)
            state[n * (TN // HD) + h] = lax.dot_general(
                k[:, cut], v[:, cut], (((0,), (0,)), ((), ())), preferred_element_type=f32
            ).astype(state.dtype)


def last_kv(part, info, xa, xb, wk, wv, acck, accv, scale):
    tok, width = acck.shape[0], acck.shape[1] // 2
    return pl.pallas_call(
        functools.partial(last_kv_kernel, part),
        out_shape=[
            pltpu.VMEM((tok, width), bf16),
            pltpu.VMEM((tok, width), bf16),
            pltpu.VMEM((width // HD, HD, HD), f32 if part == 0 else bf16),
        ],
        in_specs=[SCALARS] + [VM] * 7,
        out_specs=[VM] * 3,
        compiler_params=params(12),
        cost_estimate=cost(4 * tok * 1024 * width, 4 * MIB),
    )(info, xa, xb, wk, wv, acck, accv, scale)


def last_q_kernel(xa, xb, w, acc, scale, fq):
    half = xa.shape[1]

    @pl.loop(0, fq.shape[1] // TN)
    def _(n):
        cols = pl.ds(pl.multiple_of(n * TN, TN), TN)
        t = acc[:, cols] + dot(xa[...], w[pl.ds(0, half), cols])
        fq[:, cols] = feature((t + dot(xb[...], w[pl.ds(half, half), cols])) * scale[...])


def last_q(xa, xb, w, acc, scale):
    tok, width = acc.shape
    return pl.pallas_call(
        last_q_kernel,
        out_shape=pltpu.VMEM((tok, width), bf16),
        in_specs=[VM] * 5,
        out_specs=VM,
        compiler_params=params(12),
        cost_estimate=cost(2 * tok * 1024 * width, 4 * MIB),
    )(xa, xb, w, acc, scale)


def within_kernel(part, info, fq, fk, vb, out):
    rows, width = BLK // 2, out.shape[1]
    row = lax.broadcasted_iota(jnp.int32, (rows, rows), 0)
    col = lax.broadcasted_iota(jnp.int32, (rows, rows), 1)
    keep = row >= col
    core = 1 - info[CORE0]
    start = (core if part == 0 else 1 - core) * width

    @pl.loop(0, width // HD)
    def _(h):
        qcols = pl.ds(pl.multiple_of(start + h * HD, HD), HD)
        cols = pl.ds(pl.multiple_of(h * HD, HD), HD)

        def scores(q, k):
            return lax.dot_general(
                q, k, (((1,), (1,)), ((), ())), preferred_element_type=f32
            )

        for i in range(2):
            mine = pl.ds(i * rows, rows)
            q = fq[mine, qcols]
            s = jnp.where(keep, scores(q, fk[mine, cols]), 0.0).astype(bf16)
            y = dot(s, vb[mine, cols])
            if i == 1:
                early = pl.ds(0, rows)
                s = scores(q, fk[early, cols]).astype(bf16)
                y = y + dot(s, vb[early, cols])
            out[mine, cols] = y


def within(part, info, fq, fk, vb):
    tok, width = fk.shape
    return pl.pallas_call(
        functools.partial(within_kernel, part),
        out_shape=pltpu.VMEM((tok, width), f32),
        in_specs=[SCALARS] + [VM] * 3,
        out_specs=VM,
        compiler_params=params(12),
        cost_estimate=cost(4 * width * tok * tok, 4 * MIB),
    )(info, fq, fk, vb)


def normed(info, place, fq, ys, states, gain, o):
    rows, width = o.shape
    mine = pl.ds(pl.multiple_of(info[place] * rows, rows), rows)
    core = 1 - info[CORE0]
    for part in range(2):
        start = (core if part == 0 else 1 - core) * (width // 2)
        for g in range(width // HD // 2):
            cols = pl.ds(pl.multiple_of(start + g * HD, HD), HD)
            y = ys[part][mine, g * HD : (g + 1) * HD] + dot(fq[mine, cols], states[part][g])
            ms = jnp.mean(y * y, axis=-1, keepdims=True)
            o[:, cols] = (y * lax.rsqrt(ms + 1e-05) * gain[:, cols]).astype(bf16)


def project_out(o, wo, spans, outs):
    for (start, size), out in zip(spans, outs):

        @pl.loop(0, size // 512)
        def _(n):
            src = pl.ds(pl.multiple_of(start + n * 512, 512), 512)
            dst = pl.ds(pl.multiple_of(n * 512, 512), 512)
            out[:, dst] = dot(o[...], wo[:, src]).astype(out.dtype)


def first_kernel(place, spans, info, fq, y0, y1, own, back, gain, wo, o, *outs):
    normed(info, place, fq, (y0, y1), (own, back), gain, o)
    project_out(o, wo, spans, outs)


def first_share(info, place, spans, types, fq, y0, y1, own, back, gain, wo):
    tok, width = fq.shape
    rows = tok // 4
    return pl.pallas_call(
        functools.partial(first_kernel, place, spans),
        out_shape=[pltpu.VMEM((rows, width), bf16)]
        + [pltpu.VMEM((rows, size), t) for (_, size), t in zip(spans, types)],
        in_specs=[SCALARS] + [VM] * 7,
        out_specs=[VM] * (1 + len(spans)),
        compiler_params=params(12),
        cost_estimate=cost(2 * rows * width * sum(n for _, n in spans), 4 * MIB),
    )(info, fq, y0, y1, own, back, gain, wo)


def more_kernel(spans, o, wo, *outs):
    project_out(o, wo, spans, outs)


def more_share(spans, types, o, wo):
    rows, width = o.shape
    return pl.pallas_call(
        functools.partial(more_kernel, spans),
        out_shape=[pltpu.VMEM((rows, size), t) for (_, size), t in zip(spans, types)],
        in_specs=[VM] * 2,
        out_specs=[VM] * len(spans),
        compiler_params=params(12),
        cost_estimate=cost(2 * rows * width * sum(n for _, n in spans), 4 * MIB),
    )(o, wo)


def finish_kernel(side, own, one, two, *refs):
    out, total, sem = refs[-3:]
    half = own.shape[1]
    sums = own[...] + one[...].astype(f32) + two[...].astype(f32)
    total[...] = sums.astype(bf16)
    copy = pltpu.make_async_copy(total, out.at[:, pl.ds(side * half, half)], sem)
    copy.start()
    copy.wait()


def finish(side, own, one, two, out):
    rows, half = own.shape
    given = () if out is None else (out,)
    return pl.pallas_call(
        functools.partial(finish_kernel, side),
        out_shape=pltpu.HBM((rows, 2 * half), bf16),
        in_specs=[VM] * 3 + [HBM] * len(given),
        out_specs=HBM,
        input_output_aliases={3: 0} if given else {},
        scratch_shapes=[pltpu.VMEM((rows, half), bf16), pltpu.SemaphoreType.DMA],
        compiler_params=params(8),
        cost_estimate=cost(rows * half, 3 * MIB),
    )(own, one, two, *given)


def before_this(flags, mine, other):
    core0, core1, odd_a, high_a, first_low, early_t, early_p, all_p = flags

    def send(v, pairs):
        return shift(v.astype(bf16), pairs, "seq").astype(f32)

    theirs = send(other, SWAP)
    both = mine + theirs
    r1 = send(both, exchange(near, True))
    two = both + r1
    r2 = send(two, exchange(mirror, True))
    t3 = send(both, exchange(near, False))
    earlier = odd_a * r1 + high_a * r2
    first = core0 * earlier + core1 * (two + r2)
    r3 = send(first, exchange(near, False))
    v = first + r3 + first_low * (both + t3)
    r4 = send(v, exchange(mirror, False))
    prefix = earlier + early_p * r3 + early_t * t3 + all_p * r4
    own = (prefix + core1 * theirs).astype(bf16)
    return own, send(prefix + core0 * mine, SWAP).astype(bf16)


def on_device(codes, exponents, w_query, w_key, w_value, norm_gain, w_out):
    z = lax.axis_index("tp")
    s = lax.axis_index("seq")
    core, x, y = s % 2, (s // 2) % 4, s // 8
    first, second = jnp.where(core == 0, y, x), jnp.where(core == 0, x, y)
    info = jnp.stack([z, (z + 3) % 4, (z + 1) % 4, (z + 2) % 4, 1 - core]).astype(jnp.int32)
    core0, core1 = core == 0, core == 1
    flags = [
        v.astype(f32)
        for v in (
            core0,
            core1,
            first % 2,
            first // 2,
            core0 & (second < 2),
            core0 & (second % 2 == 1),
            core0 | (second % 2 == 1),
            core0 | (second >= 2),
        )
    ]
    _, part = codes.shape
    width = w_query.shape[1]
    half = w_out.shape[1] // 2
    scale = jnp.exp2(exponents.astype(f32))[:, None]
    gain = norm_gain.reshape(1, width)
    codes, info, *flags = lax.optimization_barrier((codes, info, *flags))
    up, down = ring(4, 1), ring(4, -1)
    weights, w_out = in_hbm(w_query, w_key, w_value), in_hbm(w_out)[0]

    a, b = split(in_hbm(codes)[0])
    a_left = shift(a, up)
    b_right = shift(b, down)
    b_left = shift(b, up)
    a_right = shift(a, down)
    a_far = shift(a_left, up)
    b_far = shift(b_right, down)

    accs = project(info, (a, b), ((OWN, 0), (OWN, 1)), weights, None)
    wq_far, wk_far, wv_far, wo = fetch(info, part, weights, w_out)
    accs = project(info, (a_left, b_right), ((LEFT, 0), (RIGHT, 1)), weights, accs)
    accs = project(info, (b_left, a_right), ((LEFT, 1), (RIGHT, 0)), weights, accs)
    last = (a_far, b_far, wk_far, wv_far, accs[1], accs[2], scale)
    k1, v1, other = last_kv(1, info, *last)
    k0, v0, mine = last_kv(0, info, *last)
    own, back = before_this(flags, mine, other)
    feat_q = last_q(a_far, b_far, wq_far, accs[0], scale)
    y0 = within(0, info, feat_q, k0, v0)
    y1 = within(1, info, feat_q, k1, v1)

    rest = (feat_q, y0, y1, own, back, gain, wo)
    o, u_far = first_share(info, FAR, ((0, half),), (bf16,), *rest)
    u_pass = shift(u_far, up)
    (l_far,) = more_share(((half, half),), (bf16,), o, wo)
    l_pass = shift(l_far, down)
    _, l_next, u_next = first_share(
        info, RIGHT, ((half, half), (0, half)), (bf16, f32), *rest
    )
    l_low = shift(l_next, up)
    _, u_prev, l_prev = first_share(info, LEFT, ((0, half), (half, half)), (bf16, f32), *rest)
    u_high = shift(u_prev, down)
    _, u, l = first_share(info, OWN, ((0, half), (half, half)), (f32, f32), *rest)
    u_low = shift((u_next + u_pass.astype(f32)).astype(bf16), up)
    l_high = shift((l_prev + l_pass.astype(f32)).astype(bf16), down)
    out = finish(0, u, u_high, u_low, None)
    return finish(1, l, l_low, l_high, out)


def solution(mesh):
    in_specs = (
        P("seq", "tp"),
        P("seq"),
        P(None, "tp"),
        P(None, "tp"),
        P(None, "tp"),
        P("tp"),
        P("tp", None),
    )
    out_specs = P(("seq", "tp"), None)

    return jax.shard_map(
        on_device, mesh=mesh, in_specs=in_specs, out_specs=out_specs, check_vma=False
    )
```

```python
import functools

import jax
import jax.numpy as jnp
from jax import lax
from jax.experimental import pallas as pl
from jax.experimental.pallas import tpu as pltpu
from jax.sharding import PartitionSpec as P

HD = 128
BLK = 512
TN = 256
MIB = 1 << 20


f32 = jnp.float32
bf16 = jnp.bfloat16
HBM = pl.BlockSpec(memory_space=pltpu.HBM)
VM = pl.BlockSpec(memory_space=pltpu.VMEM)


def ring(n, d):
    return [(i, (i + d) % n) for i in range(n)]


def chip(y, x, c):
    return (y * 4 + x) * 2 + c


def turn(k, first):
    found = []
    for y in range(4):
        for x in range(4):
            for c in range(2):
                along_y = (c == 0) == first
                to = ((y + k) % 4, x, c) if along_y else (y, (x + k) % 4, c)
                found.append((chip(y, x, c), chip(*to)))
    return found


SWAP = [(s, s ^ 1) for s in range(32)]


def shift(v, pairs, axis="tp"):
    return lax.ppermute(v, axis, pairs)


def in_hbm(*arrays):
    return [pltpu.with_memory_space_constraint(v, pltpu.HBM) for v in arrays]


def dot(a, b):
    return jnp.dot(a, b, preferred_element_type=f32)


def params(limit, **more):
    return pltpu.CompilerParams(vmem_limit_bytes=limit * MIB, **more)


def cost(flops, nbytes):
    return pl.CostEstimate(flops=flops, bytes_accessed=nbytes, transcendentals=0)


OWN, LEFT, RIGHT, FAR, CORE0 = range(5)
SCALARS = pl.BlockSpec(memory_space=pltpu.SMEM)


def project_kernel(count, have, info, *refs):
    xs, refs = refs[:count], refs[count:]
    ws, refs = refs[: 3 * count], refs[3 * count :]
    accs, outs = (refs[:3], refs[3:]) if have else (None, refs)
    cols = pl.ds(pl.multiple_of(pl.program_id(0) * TN, TN), TN)
    for i in range(3):
        total = accs[i][:, cols] if have else None
        for j in range(count):
            term = dot(xs[j][...], ws[3 * j + i][...])
            total = term if total is None else total + term
        outs[i][:, cols] = total


def project(info, pieces, blocks, weights, accs):
    count, have = len(pieces), accs is not None
    tok, depth = pieces[0].shape
    width = weights[0].shape[1]

    def wspec(j):
        device, half = blocks[j]
        return pl.BlockSpec((depth, TN), lambda n, i: (2 * i[device] + half, n))

    return pl.pallas_call(
        functools.partial(project_kernel, count, have),
        out_shape=[pltpu.VMEM((tok, width), f32)] * 3,
        grid_spec=pltpu.PrefetchScalarGridSpec(
            num_scalar_prefetch=1,
            grid=(width // TN,),
            in_specs=[VM] * count
            + [wspec(j) for j in range(count) for _ in range(3)]
            + ([VM] * 3 if have else []),
            out_specs=[VM] * 3,
        ),
        compiler_params=params(16),
        cost_estimate=cost(6 * count * tok * depth * width, 6 * count * depth * width),
    )(info, *pieces, *(list(weights) * count), *(accs or ()))


def split_kernel(codes, a, b, sem):
    half = a.shape[1]
    copies = [
        pltpu.make_async_copy(codes.at[:, pl.ds(0, half)], a, sem.at[0]),
        pltpu.make_async_copy(codes.at[:, pl.ds(half, half)], b, sem.at[1]),
    ]
    for c in copies:
        c.start()
    for c in copies:
        c.wait()


def split(codes):
    tok, part = codes.shape
    return pl.pallas_call(
        split_kernel,
        out_shape=[pltpu.VMEM((tok, part // 2), bf16)] * 2,
        in_specs=[HBM],
        out_specs=[VM] * 2,
        scratch_shapes=[pltpu.SemaphoreType.DMA((2,))],
        compiler_params=params(4),
        cost_estimate=cost(0, 2 * MIB),
    )(codes)


def fetch_kernel(rows, info, wq, wk, wv, wo, fq, fk, fv, fo, sem):
    start = pl.multiple_of(info[FAR] * rows, rows)
    copies = [
        pltpu.make_async_copy(w.at[pl.ds(start, rows), :], f, sem.at[n])
        for n, (w, f) in enumerate(((wk, fk), (wv, fv), (wq, fq)))
    ]
    copies.append(pltpu.make_async_copy(wo, fo, sem.at[3]))
    for c in copies:
        c.start()
    for c in copies:
        c.wait()


def fetch(info, rows, weights, w_out):
    width = weights[0].shape[1]
    return pl.pallas_call(
        functools.partial(fetch_kernel, rows),
        out_shape=[pltpu.VMEM((rows, width), bf16)] * 3 + [pltpu.VMEM(w_out.shape, bf16)],
        in_specs=[SCALARS] + [HBM] * 4,
        out_specs=[VM] * 4,
        scratch_shapes=[pltpu.SemaphoreType.DMA((4,))],
        compiler_params=params(8),
        cost_estimate=cost(0, 14 * MIB),
    )(info, *weights, w_out)


def feature(t):
    return jnp.where(t > 0, t + 1.0, jnp.exp(t)).astype(bf16)


def last_kv_kernel(part, info, xa, xb, wk, wv, acck, accv, scale, fk, vb, state):
    half, width = xa.shape[1], fk.shape[1]
    core = 1 - info[CORE0]
    start = (core if part == 0 else 1 - core) * width

    for n in range(width // TN):
        cols = pl.ds(pl.multiple_of(start + n * TN, TN), TN)
        ocols = slice(n * TN, (n + 1) * TN)

        def full(w, acc):
            t = acc[:, cols] + dot(xa[...], w[pl.ds(0, half), cols])
            return (t + dot(xb[...], w[pl.ds(half, half), cols])) * scale[...]

        k = feature(full(wk, acck))
        v = full(wv, accv).astype(bf16)
        fk[:, ocols] = k
        vb[:, ocols] = v
        for h in range(TN // HD):
            cut = slice(h * HD, (h + 1) * HD)
            state[n * (TN // HD) + h] = lax.dot_general(
                k[:, cut], v[:, cut], (((0,), (0,)), ((), ())), preferred_element_type=f32
            ).astype(state.dtype)


def last_kv(part, info, xa, xb, wk, wv, acck, accv, scale):
    tok, width = acck.shape[0], acck.shape[1] // 2
    return pl.pallas_call(
        functools.partial(last_kv_kernel, part),
        out_shape=[
            pltpu.VMEM((tok, width), bf16),
            pltpu.VMEM((tok, width), bf16),
            pltpu.VMEM((width // HD, HD, HD), f32 if part == 0 else bf16),
        ],
        in_specs=[SCALARS] + [VM] * 7,
        out_specs=[VM] * 3,
        compiler_params=params(12),
        cost_estimate=cost(4 * tok * 1024 * width, 4 * MIB),
    )(info, xa, xb, wk, wv, acck, accv, scale)


def last_q_kernel(xa, xb, w, acc, scale, fq):
    half = xa.shape[1]

    @pl.loop(0, fq.shape[1] // TN)
    def _(n):
        cols = pl.ds(pl.multiple_of(n * TN, TN), TN)
        t = acc[:, cols] + dot(xa[...], w[pl.ds(0, half), cols])
        fq[:, cols] = feature((t + dot(xb[...], w[pl.ds(half, half), cols])) * scale[...])


def last_q(xa, xb, w, acc, scale):
    tok, width = acc.shape
    return pl.pallas_call(
        last_q_kernel,
        out_shape=pltpu.VMEM((tok, width), bf16),
        in_specs=[VM] * 5,
        out_specs=VM,
        compiler_params=params(12),
        cost_estimate=cost(2 * tok * 1024 * width, 4 * MIB),
    )(xa, xb, w, acc, scale)


def within_kernel(part, info, fq, fk, vb, out):
    rows, width = BLK // 2, out.shape[1]
    row = lax.broadcasted_iota(jnp.int32, (rows, rows), 0)
    col = lax.broadcasted_iota(jnp.int32, (rows, rows), 1)
    keep = row >= col
    core = 1 - info[CORE0]
    start = (core if part == 0 else 1 - core) * width

    @pl.loop(0, width // HD)
    def _(h):
        qcols = pl.ds(pl.multiple_of(start + h * HD, HD), HD)
        cols = pl.ds(pl.multiple_of(h * HD, HD), HD)

        def scores(q, k):
            return lax.dot_general(
                q, k, (((1,), (1,)), ((), ())), preferred_element_type=f32
            )

        for i in range(2):
            mine = pl.ds(i * rows, rows)
            q = fq[mine, qcols]
            s = jnp.where(keep, scores(q, fk[mine, cols]), 0.0).astype(bf16)
            y = dot(s, vb[mine, cols])
            if i == 1:
                early = pl.ds(0, rows)
                s = scores(q, fk[early, cols]).astype(bf16)
                y = y + dot(s, vb[early, cols])
            out[mine, cols] = y


def within(part, info, fq, fk, vb):
    tok, width = fk.shape
    return pl.pallas_call(
        functools.partial(within_kernel, part),
        out_shape=pltpu.VMEM((tok, width), f32),
        in_specs=[SCALARS] + [VM] * 3,
        out_specs=VM,
        compiler_params=params(12),
        cost_estimate=cost(4 * width * tok * tok, 4 * MIB),
    )(info, fq, fk, vb)


def normed(info, place, fq, ys, states, gain, o):
    rows, width = o.shape
    mine = pl.ds(pl.multiple_of(info[place] * rows, rows), rows)
    core = 1 - info[CORE0]
    for part in range(2):
        start = (core if part == 0 else 1 - core) * (width // 2)
        for g in range(width // HD // 2):
            cols = pl.ds(pl.multiple_of(start + g * HD, HD), HD)
            y = ys[part][mine, g * HD : (g + 1) * HD] + dot(fq[mine, cols], states[part][g])
            ms = jnp.mean(y * y, axis=-1, keepdims=True)
            o[:, cols] = (y * lax.rsqrt(ms + 1e-05) * gain[:, cols]).astype(bf16)


def project_out(o, wo, spans, outs):
    for (start, size), out in zip(spans, outs):

        @pl.loop(0, size // 512)
        def _(n):
            src = pl.ds(pl.multiple_of(start + n * 512, 512), 512)
            dst = pl.ds(pl.multiple_of(n * 512, 512), 512)
            out[:, dst] = dot(o[...], wo[:, src]).astype(out.dtype)


def first_kernel(place, spans, info, fq, y0, y1, own, back, gain, wo, o, *outs):
    normed(info, place, fq, (y0, y1), (own, back), gain, o)
    project_out(o, wo, spans, outs)


def first_share(info, place, spans, types, fq, y0, y1, own, back, gain, wo):
    tok, width = fq.shape
    rows = tok // 4
    return pl.pallas_call(
        functools.partial(first_kernel, place, spans),
        out_shape=[pltpu.VMEM((rows, width), bf16)]
        + [pltpu.VMEM((rows, size), t) for (_, size), t in zip(spans, types)],
        in_specs=[SCALARS] + [VM] * 7,
        out_specs=[VM] * (1 + len(spans)),
        compiler_params=params(12),
        cost_estimate=cost(2 * rows * width * sum(n for _, n in spans), 4 * MIB),
    )(info, fq, y0, y1, own, back, gain, wo)


def more_kernel(spans, o, wo, *outs):
    project_out(o, wo, spans, outs)


def more_share(spans, types, o, wo):
    rows, width = o.shape
    return pl.pallas_call(
        functools.partial(more_kernel, spans),
        out_shape=[pltpu.VMEM((rows, size), t) for (_, size), t in zip(spans, types)],
        in_specs=[VM] * 2,
        out_specs=[VM] * len(spans),
        compiler_params=params(12),
        cost_estimate=cost(2 * rows * width * sum(n for _, n in spans), 4 * MIB),
    )(o, wo)


def finish_kernel(side, own, one, two, *refs):
    out, total, sem = refs[-3:]
    half = own.shape[1]
    sums = own[...] + one[...].astype(f32) + two[...].astype(f32)
    total[...] = sums.astype(bf16)
    copy = pltpu.make_async_copy(total, out.at[:, pl.ds(side * half, half)], sem)
    copy.start()
    copy.wait()


def finish(side, own, one, two, out):
    rows, half = own.shape
    given = () if out is None else (out,)
    return pl.pallas_call(
        functools.partial(finish_kernel, side),
        out_shape=pltpu.HBM((rows, 2 * half), bf16),
        in_specs=[VM] * 3 + [HBM] * len(given),
        out_specs=HBM,
        input_output_aliases={3: 0} if given else {},
        scratch_shapes=[pltpu.VMEM((rows, half), bf16), pltpu.SemaphoreType.DMA],
        compiler_params=params(8),
        cost_estimate=cost(rows * half, 3 * MIB),
    )(own, one, two, *given)


def before_this(flags, mine, other):
    core0, core1, seen_a, later_b, seen_b = flags[0], flags[1], flags[2:5], flags[5:8], flags[8:]

    def send(v, pairs):
        return shift(v.astype(bf16), pairs, "seq").astype(f32)

    theirs = send(other, SWAP)
    both = mine + theirs
    r = {k: send(both, turn(k, True)) for k in (2, 1, 3)}
    earlier = seen_a[0] * r[1] + seen_a[1] * r[2] + seen_a[2] * r[3]
    total = core0 * earlier + core1 * (both + r[1] + r[2] + r[3])
    t = {k: send(total + later_b[k - 1] * both, turn(k, False)) for k in (2, 1, 3)}
    prefix = earlier + seen_b[0] * t[1] + seen_b[1] * t[2] + seen_b[2] * t[3]
    own = (prefix + core1 * theirs).astype(bf16)
    return own, send(prefix + core0 * mine, SWAP).astype(bf16)


def on_device(codes, exponents, w_query, w_key, w_value, norm_gain, w_out):
    z = lax.axis_index("tp")
    s = lax.axis_index("seq")
    core, x, y = s % 2, (s // 2) % 4, s // 8
    first, second = jnp.where(core == 0, y, x), jnp.where(core == 0, x, y)
    info = jnp.stack([z, (z + 3) % 4, (z + 1) % 4, (z + 2) % 4, 1 - core]).astype(jnp.int32)
    core0, core1 = core == 0, core == 1
    flags = [core0, core1]
    flags += [first >= k for k in (1, 2, 3)]
    flags += [core0 & (second < 4 - k) for k in (1, 2, 3)]
    flags += [core0 | (second >= k) for k in (1, 2, 3)]
    flags = [v.astype(f32) for v in flags]
    _, part = codes.shape
    width = w_query.shape[1]
    half = w_out.shape[1] // 2
    scale = jnp.exp2(exponents.astype(f32))[:, None]
    gain = norm_gain.reshape(1, width)
    codes, info, *flags = lax.optimization_barrier((codes, info, *flags))
    up, down = ring(4, 1), ring(4, -1)
    weights, w_out = in_hbm(w_query, w_key, w_value), in_hbm(w_out)[0]

    a, b = split(in_hbm(codes)[0])
    a_left = shift(a, up)
    b_right = shift(b, down)
    b_left = shift(b, up)
    a_right = shift(a, down)
    a_far = shift(a_left, up)
    b_far = shift(b_right, down)

    accs = project(info, (a, b), ((OWN, 0), (OWN, 1)), weights, None)
    wq_far, wk_far, wv_far, wo = fetch(info, part, weights, w_out)
    accs = project(info, (a_left, b_right), ((LEFT, 0), (RIGHT, 1)), weights, accs)
    accs = project(info, (b_left, a_right), ((LEFT, 1), (RIGHT, 0)), weights, accs)
    last = (a_far, b_far, wk_far, wv_far, accs[1], accs[2], scale)
    k1, v1, other = last_kv(1, info, *last)
    k0, v0, mine = last_kv(0, info, *last)
    own, back = before_this(flags, mine, other)
    feat_q = last_q(a_far, b_far, wq_far, accs[0], scale)
    y0 = within(0, info, feat_q, k0, v0)
    y1 = within(1, info, feat_q, k1, v1)

    rest = (feat_q, y0, y1, own, back, gain, wo)
    o, u_far = first_share(info, FAR, ((0, half),), (bf16,), *rest)
    u_pass = shift(u_far, up)
    (l_far,) = more_share(((half, half),), (bf16,), o, wo)
    l_pass = shift(l_far, down)
    _, l_next, u_next = first_share(
        info, RIGHT, ((half, half), (0, half)), (bf16, f32), *rest
    )
    l_low = shift(l_next, up)
    _, u_prev, l_prev = first_share(info, LEFT, ((0, half), (half, half)), (bf16, f32), *rest)
    u_high = shift(u_prev, down)
    _, u, l = first_share(info, OWN, ((0, half), (half, half)), (f32, f32), *rest)
    u_low = shift((u_next + u_pass.astype(f32)).astype(bf16), up)
    l_high = shift((l_prev + l_pass.astype(f32)).astype(bf16), down)
    out = finish(0, u, u_high, u_low, None)
    return finish(1, l, l_low, l_high, out)


def solution(mesh):
    in_specs = (
        P("seq", "tp"),
        P("seq"),
        P(None, "tp"),
        P(None, "tp"),
        P(None, "tp"),
        P("tp"),
        P("tp", None),
    )
    out_specs = P(("seq", "tp"), None)

    return jax.shard_map(
        on_device, mesh=mesh, in_specs=in_specs, out_specs=out_specs, check_vma=False
    )
```

```python
import functools

import jax
import jax.numpy as jnp
from jax import lax
from jax.experimental import pallas as pl
from jax.experimental.pallas import tpu as pltpu
from jax.sharding import PartitionSpec as P

HD = 128
TN = 256
MIB = 1 << 20


f32 = jnp.float32
bf16 = jnp.bfloat16
HBM = pl.BlockSpec(memory_space=pltpu.HBM)
VM = pl.BlockSpec(memory_space=pltpu.VMEM)


def ring(n, d):
    return [(i, (i + d) % n) for i in range(n)]


def chip(y, x, c):
    return (y * 4 + x) * 2 + c


def turn(k, first):
    found = []
    for y in range(4):
        for x in range(4):
            for c in range(2):
                along_y = (c == 0) == first
                to = ((y + k) % 4, x, c) if along_y else (y, (x + k) % 4, c)
                found.append((chip(y, x, c), chip(*to)))
    return found


SWAP = [(s, s ^ 1) for s in range(32)]


def shift(v, pairs, axis="tp"):
    return lax.ppermute(v, axis, pairs)


def in_hbm(*arrays):
    return [pltpu.with_memory_space_constraint(v, pltpu.HBM) for v in arrays]


def dot(a, b):
    return jnp.dot(a, b, preferred_element_type=f32)


def params(limit, **more):
    return pltpu.CompilerParams(vmem_limit_bytes=limit * MIB, **more)


def cost(flops, nbytes):
    return pl.CostEstimate(flops=flops, bytes_accessed=nbytes, transcendentals=0)


OWN, LEFT, RIGHT, FAR, CORE0 = range(5)
SCALARS = pl.BlockSpec(memory_space=pltpu.SMEM)


def project_kernel(count, have, riders, info, *refs):
    xs, refs = refs[:count], refs[count:]
    ws, refs = refs[: 3 * count], refs[3 * count :]
    accs, refs = (refs[:3], refs[3:]) if have else (None, refs)
    wide, refs = refs[: len(riders)], refs[len(riders) :]
    outs, refs = refs[:3], refs[3:]
    step = pl.program_id(0)
    copies = []
    for n, (place, col) in enumerate(riders):
        rows, columns = refs[n].shape
        begin = 0 if place is None else pl.multiple_of(info[place] * rows, rows)
        source = wide[n].at[pl.ds(begin, rows), pl.ds(col, columns)]
        copies.append(pltpu.make_async_copy(source, refs[n], refs[-1].at[n]))

    @pl.when(step == 0)
    def _():
        for c in copies:
            c.start()

    cols = pl.ds(pl.multiple_of(step * TN, TN), TN)
    for i in range(3):
        total = accs[i][:, cols] if have else None
        for j in range(count):
            term = dot(xs[j][...], ws[3 * j + i][...])
            total = term if total is None else total + term
        outs[i][:, cols] = total

    @pl.when(step == pl.num_programs(0) - 1)
    def _():
        for c in copies:
            c.wait()


def project(info, pieces, blocks, weights, accs, riders=()):
    count, have = len(pieces), accs is not None
    tok, depth = pieces[0].shape
    width = weights[0].shape[1]

    def wspec(j):
        device, half = blocks[j]
        return pl.BlockSpec((depth, TN), lambda n, i: (2 * i[device] + half, n))

    plan = [(place, col) for _, place, col, _ in riders]
    found = pl.pallas_call(
        functools.partial(project_kernel, count, have, plan),
        out_shape=[pltpu.VMEM((tok, width), f32)] * 3
        + [pltpu.VMEM(shape, bf16) for _, _, _, shape in riders],
        grid_spec=pltpu.PrefetchScalarGridSpec(
            num_scalar_prefetch=1,
            grid=(width // TN,),
            in_specs=[VM] * count
            + [wspec(j) for j in range(count) for _ in range(3)]
            + ([VM] * 3 if have else [])
            + [HBM] * len(riders),
            out_specs=[VM] * (3 + len(riders)),
            scratch_shapes=[pltpu.SemaphoreType.DMA((max(len(riders), 1),))],
        ),
        compiler_params=params(16),
        cost_estimate=cost(6 * count * tok * depth * width, 6 * count * depth * width),
    )(info, *pieces, *(list(weights) * count), *(accs or ()), *(w for w, _, _, _ in riders))
    return found[:3], found[3:]


def split_kernel(codes, a, b, sem):
    half = a.shape[1]
    copies = [
        pltpu.make_async_copy(codes.at[:, pl.ds(0, half)], a, sem.at[0]),
        pltpu.make_async_copy(codes.at[:, pl.ds(half, half)], b, sem.at[1]),
    ]
    for c in copies:
        c.start()
    for c in copies:
        c.wait()


def split(codes):
    tok, part = codes.shape
    return pl.pallas_call(
        split_kernel,
        out_shape=[pltpu.VMEM((tok, part // 2), bf16)] * 2,
        in_specs=[HBM],
        out_specs=[VM] * 2,
        scratch_shapes=[pltpu.SemaphoreType.DMA((2,))],
        compiler_params=params(4),
        cost_estimate=cost(0, 2 * MIB),
    )(codes)


def feature(t):
    return jnp.where(t > 0, t + 1.0, jnp.exp(t)).astype(bf16)


def last_terms(xa, xb, w, acc, scale, rows, cols):
    half = xa.shape[1]
    t = acc[rows, cols] + dot(xa[...], w[pl.ds(0, half), cols])
    return (t + dot(xb[...], w[pl.ds(half, half), cols])) * scale[rows, :]


def own_state(k, v):
    return lax.dot_general(k, v, (((0,), (0,)), ((), ())), preferred_element_type=f32)


def early_kv_kernel(xa, xb, wk, wv, acck, accv, scale, wide, fk, vb, state, near, sem):
    copy = pltpu.make_async_copy(wide.at[:, pl.ds(0, near.shape[1])], near, sem)
    copy.start()
    rows = slice(0, fk.shape[0])
    for n in range(fk.shape[1] // TN):
        cols = slice(n * TN, (n + 1) * TN)
        k = feature(last_terms(xa, xb, wk, acck, scale, rows, cols))
        v = last_terms(xa, xb, wv, accv, scale, rows, cols).astype(bf16)
        fk[:, cols] = k
        vb[:, cols] = v
        for h in range(TN // HD):
            cut = slice(h * HD, (h + 1) * HD)
            state[n * (TN // HD) + h] = own_state(k[:, cut], v[:, cut])
    copy.wait()


def early_kv(xa, xb, wk, wv, acck, accv, scale, w_out):
    tok, width = xa.shape[0], acck.shape[1]
    return pl.pallas_call(
        early_kv_kernel,
        out_shape=[
            pltpu.VMEM((tok, width), bf16),
            pltpu.VMEM((tok, width), bf16),
            pltpu.VMEM((width // HD, HD, HD), f32),
            pltpu.VMEM((w_out.shape[0], w_out.shape[1] // 2), bf16),
        ],
        in_specs=[VM] * 7 + [HBM],
        out_specs=[VM] * 4,
        scratch_shapes=[pltpu.SemaphoreType.DMA],
        compiler_params=params(12),
        cost_estimate=cost(4 * tok * 1024 * width, 4 * MIB),
    )(xa, xb, wk, wv, acck, accv, scale, w_out)


def late_kv_kernel(part, info, xa, xb, wk, wv, acck, accv, scale, early, fk, vb, state):
    tok, width = fk.shape
    core = 1 - info[CORE0]
    place = core if part == 0 else 1 - core
    rows = slice(tok, 2 * tok)
    for n in range(width // TN):
        cols = pl.ds(pl.multiple_of(place * width + n * TN, TN), TN)
        ocols = slice(n * TN, (n + 1) * TN)
        k = feature(last_terms(xa, xb, wk, acck, scale, rows, cols))
        v = last_terms(xa, xb, wv, accv, scale, rows, cols).astype(bf16)
        fk[:, ocols] = k
        vb[:, ocols] = v
        for h in range(TN // HD):
            cut = slice(h * HD, (h + 1) * HD)
            at = n * (TN // HD) + h
            total = early[place * (width // HD) + at] + own_state(k[:, cut], v[:, cut])
            state[at] = total.astype(state.dtype)


def late_kv(part, info, xa, xb, wk, wv, acck, accv, scale, early):
    tok, width = xa.shape[0], acck.shape[1] // 2
    return pl.pallas_call(
        functools.partial(late_kv_kernel, part),
        out_shape=[
            pltpu.VMEM((tok, width), bf16),
            pltpu.VMEM((tok, width), bf16),
            pltpu.VMEM((width // HD, HD, HD), f32 if part == 0 else bf16),
        ],
        in_specs=[SCALARS] + [VM] * 8,
        out_specs=[VM] * 3,
        compiler_params=params(12),
        cost_estimate=cost(4 * tok * 1024 * width, 4 * MIB),
    )(info, xa, xb, wk, wv, acck, accv, scale, early)


def last_q_kernel(xa1, xa2, xb1, xb2, w, acc, scale, fq):
    tok = xa1.shape[0]
    for n in range(fq.shape[1] // TN):
        cols = slice(n * TN, (n + 1) * TN)
        for i, (xa, xb) in enumerate(((xa1, xb1), (xa2, xb2))):
            rows = slice(i * tok, (i + 1) * tok)
            fq[rows, cols] = feature(last_terms(xa, xb, w, acc, scale, rows, cols))


def last_q(xa, xb, w, acc, scale):
    tok, width = acc.shape
    return pl.pallas_call(
        last_q_kernel,
        out_shape=pltpu.VMEM((tok, width), bf16),
        in_specs=[VM] * 7,
        out_specs=VM,
        compiler_params=params(12),
        cost_estimate=cost(2 * tok * 1024 * width, 4 * MIB),
    )(*xa, *xb, w, acc, scale)


def within_kernel(part, info, fq, k_early, v_early, k_late, v_late, out):
    rows, width = k_late.shape
    row = lax.broadcasted_iota(jnp.int32, (rows, rows), 0)
    col = lax.broadcasted_iota(jnp.int32, (rows, rows), 1)
    keep = row >= col
    core = 1 - info[CORE0]
    start = (core if part == 0 else 1 - core) * width

    def scores(q, k):
        return lax.dot_general(q, k, (((1,), (1,)), ((), ())), preferred_element_type=f32)

    def masked(q, k):
        return jnp.where(keep, scores(q, k), 0.0).astype(bf16)

    for h in range(width // HD):
        qcols = pl.ds(pl.multiple_of(start + h * HD, HD), HD)
        cols = slice(h * HD, (h + 1) * HD)
        k, v = k_early[:, qcols], v_early[:, qcols]
        q = fq[0:rows, qcols]
        out[0:rows, cols] = dot(masked(q, k), v)
        q = fq[rows : 2 * rows, qcols]
        y = dot(scores(q, k).astype(bf16), v)
        out[rows : 2 * rows, cols] = y + dot(masked(q, k_late[:, cols]), v_late[:, cols])


def within(part, info, fq, *keys):
    tok, width = fq.shape[0], fq.shape[1] // 2
    return pl.pallas_call(
        functools.partial(within_kernel, part),
        out_shape=pltpu.VMEM((tok, width), f32),
        in_specs=[SCALARS] + [VM] * 5,
        out_specs=VM,
        compiler_params=params(12),
        cost_estimate=cost(4 * width * tok * tok, 4 * MIB),
    )(info, fq, *keys)


def normed(info, place, fq, ys, states, gain, o):
    rows, width = o.shape
    mine = pl.ds(pl.multiple_of(info[place] * rows, rows), rows)
    core = 1 - info[CORE0]
    for part in range(2):
        start = (core if part == 0 else 1 - core) * (width // 2)
        for g in range(width // HD // 2):
            cols = pl.ds(pl.multiple_of(start + g * HD, HD), HD)
            y = ys[part][mine, g * HD : (g + 1) * HD] + dot(fq[mine, cols], states[part][g])
            ms = jnp.mean(y * y, axis=-1, keepdims=True)
            o[:, cols] = (y * lax.rsqrt(ms + 1e-05) * gain[:, cols]).astype(bf16)


def project_out(o, wos, outs):
    for wo, out in zip(wos, outs):

        @pl.loop(0, out.shape[1] // 512)
        def _(n):
            cols = pl.ds(pl.multiple_of(n * 512, 512), 512)
            out[:, cols] = dot(o[...], wo[:, cols]).astype(out.dtype)


def first_kernel(place, sides, info, fq, y0, y1, own, back, gain, *refs):
    normed(info, place, fq, (y0, y1), (own, back), gain, refs[sides])
    project_out(refs[sides], refs[:sides], refs[sides + 1 :])


def first_share(info, place, wos, types, fq, y0, y1, own, back, gain):
    tok, width = fq.shape
    rows, half = tok // 4, wos[0].shape[1]
    return pl.pallas_call(
        functools.partial(first_kernel, place, len(wos)),
        out_shape=[pltpu.VMEM((rows, width), bf16)] + [pltpu.VMEM((rows, half), t) for t in types],
        in_specs=[SCALARS] + [VM] * (6 + len(wos)),
        out_specs=[VM] * (1 + len(wos)),
        compiler_params=params(12),
        cost_estimate=cost(2 * rows * width * half * len(wos), 4 * MIB),
    )(info, fq, y0, y1, own, back, gain, *wos)


def more_kernel(o, wo, out):
    project_out(o, (wo,), (out,))


def more_share(o, wo):
    rows, half = o.shape[0], wo.shape[1]
    return pl.pallas_call(
        more_kernel,
        out_shape=pltpu.VMEM((rows, half), bf16),
        in_specs=[VM] * 2,
        out_specs=VM,
        compiler_params=params(12),
        cost_estimate=cost(2 * rows * o.shape[1] * half, 4 * MIB),
    )(o, wo)


def finish_kernel(side, own, one, two, *refs):
    out, total, sem = refs[-3:]
    half = own.shape[1]
    sums = own[...] + one[...].astype(f32) + two[...].astype(f32)
    total[...] = sums.astype(bf16)
    copy = pltpu.make_async_copy(total, out.at[:, pl.ds(side * half, half)], sem)
    copy.start()
    copy.wait()


def finish(side, own, one, two, out):
    rows, half = own.shape
    given = () if out is None else (out,)
    return pl.pallas_call(
        functools.partial(finish_kernel, side),
        out_shape=pltpu.HBM((rows, 2 * half), bf16),
        in_specs=[VM] * 3 + [HBM] * len(given),
        out_specs=HBM,
        input_output_aliases={3: 0} if given else {},
        scratch_shapes=[pltpu.VMEM((rows, half), bf16), pltpu.SemaphoreType.DMA],
        compiler_params=params(8),
        cost_estimate=cost(rows * half, 3 * MIB),
    )(own, one, two, *given)


def before_this(flags, mine, other):
    core0, core1, seen_a, later_b, seen_b = flags[0], flags[1], flags[2:5], flags[5:8], flags[8:]

    def send(v, pairs):
        return shift(v.astype(bf16), pairs, "seq").astype(f32)

    theirs = send(other, SWAP)
    both = mine + theirs
    r = {k: send(both, turn(k, True)) for k in (2, 1, 3)}
    earlier = seen_a[0] * r[1] + seen_a[1] * r[2] + seen_a[2] * r[3]
    total = core0 * earlier + core1 * (both + r[1] + r[2] + r[3])
    t = {k: send(total + later_b[k - 1] * both, turn(k, False)) for k in (2, 1, 3)}
    prefix = earlier + seen_b[0] * t[1] + seen_b[1] * t[2] + seen_b[2] * t[3]
    own = (prefix + core1 * theirs).astype(bf16)
    return own, send(prefix + core0 * mine, SWAP).astype(bf16)


def on_device(codes, exponents, w_query, w_key, w_value, norm_gain, w_out):
    z = lax.axis_index("tp")
    s = lax.axis_index("seq")
    core, x, y = s % 2, (s // 2) % 4, s // 8
    first, second = jnp.where(core == 0, y, x), jnp.where(core == 0, x, y)
    info = jnp.stack([z, (z + 3) % 4, (z + 1) % 4, (z + 2) % 4, 1 - core]).astype(jnp.int32)
    core0, core1 = core == 0, core == 1
    flags = [core0, core1]
    flags += [first >= k for k in (1, 2, 3)]
    flags += [core0 & (second < 4 - k) for k in (1, 2, 3)]
    flags += [core0 | (second >= k) for k in (1, 2, 3)]
    flags = [v.astype(f32) for v in flags]
    tok, part = codes.shape
    width = w_query.shape[1]
    half = w_out.shape[1] // 2
    scale = jnp.exp2(exponents.astype(f32))[:, None]
    gain = norm_gain.reshape(1, width)
    codes, info, *flags = lax.optimization_barrier((codes, info, *flags))
    up, down = ring(4, 1), ring(4, -1)
    weights, w_out = in_hbm(w_query, w_key, w_value), in_hbm(w_out)[0]

    a, b = split(in_hbm(codes)[0])
    a_left = shift(a, up)
    b_right = shift(b, down)
    b_left = shift(b, up)
    a_right = shift(a, down)
    early = tok // 2
    a_far1 = shift(a_left[:early], up)
    b_far1 = shift(b_right[:early], down)
    a_far2 = shift(a_left[early:], up)
    b_far2 = shift(b_right[early:], down)

    accs, (wk_far, wv_far, wq_far) = project(
        info,
        (a, b),
        ((OWN, 0), (OWN, 1)),
        weights,
        None,
        [(weights[n], FAR, 0, (part, width)) for n in (1, 2, 0)],
    )
    accs, (wo_l,) = project(
        info,
        (a_left, b_right),
        ((LEFT, 0), (RIGHT, 1)),
        weights,
        accs,
        [(w_out, None, half, (w_out.shape[0], half))],
    )
    accs, _ = project(info, (b_left, a_right), ((LEFT, 1), (RIGHT, 0)), weights, accs)
    last = (wk_far, wv_far, accs[1], accs[2], scale)
    k_early, v_early, state, wo_u = early_kv(a_far1, b_far1, *last, w_out)
    k1, v1, other = late_kv(1, info, a_far2, b_far2, *last, state)
    k0, v0, mine = late_kv(0, info, a_far2, b_far2, *last, state)
    own, back = before_this(flags, mine, other)
    feat_q = last_q((a_far1, a_far2), (b_far1, b_far2), wq_far, accs[0], scale)
    y0 = within(0, info, feat_q, k_early, v_early, k0, v0)
    y1 = within(1, info, feat_q, k_early, v_early, k1, v1)

    rest = (feat_q, y0, y1, own, back, gain)
    o, u_far = first_share(info, FAR, (wo_u,), (bf16,), *rest)
    u_pass = shift(u_far, up)
    l_pass = shift(more_share(o, wo_l), down)
    _, l_next, u_next = first_share(info, RIGHT, (wo_l, wo_u), (bf16, f32), *rest)
    l_low = shift(l_next, up)
    _, u_prev, l_prev = first_share(info, LEFT, (wo_u, wo_l), (bf16, f32), *rest)
    u_high = shift(u_prev, down)
    _, u, l = first_share(info, OWN, (wo_u, wo_l), (f32, f32), *rest)
    u_low = shift((u_next + u_pass.astype(f32)).astype(bf16), up)
    l_high = shift((l_prev + l_pass.astype(f32)).astype(bf16), down)
    out = finish(0, u, u_high, u_low, None)
    return finish(1, l, l_low, l_high, out)


def solution(mesh):
    in_specs = (
        P("seq", "tp"),
        P("seq"),
        P(None, "tp"),
        P(None, "tp"),
        P(None, "tp"),
        P("tp"),
        P("tp", None),
    )
    out_specs = P(("seq", "tp"), None)

    return jax.shard_map(
        on_device, mesh=mesh, in_specs=in_specs, out_specs=out_specs, check_vma=False
    )
```
